256 devices in a mesh: dp: 32 (over y, z), cent: 8 (over x, core).
Axes of the slice: x: 4, y: 4, z: 8, core: 2. Of those that a mesh axis runs over, the one named last changes fastest.
Arguments:
- embeddings: bfloat16 [16384, 768], P('dp'), may hold values from -400 to 400, as said below
- centroids: bfloat16 [16384, 768], P('cent'), may hold values from -400 to 400, as said below
Outputs:
- new_centroids: float32 [16384, 768], P(('cent', 'dp'))
The draws below stay inside these ranges and needn't reach their ends.
Inputs may be any that keep to these rules, and one draw needn't show every extreme that they name: `embeddings`: finite real values. `centroids`: finite real values.
All inputs are finite; a program needn't handle non-finite values.
Results may differ from the reference program's by a relative error of at most 0.0038.
Values sent between devices are 32-bit elements; how exact they have to be, the bound alone decides.
A program may use at most 64 MiB of HBM per device.

```python
import math
import jax
import jax.numpy as jnp
from jax import lax

FEATURE_DIM = 768
ROUNDS = 2
K = 16384
N = 16384


def shared_parts(key):
    col_scale = jnp.exp(jax.random.uniform(jax.random.fold_in(key, 101), (FEATURE_DIM,), jnp.float32, 0.0, math.log(10.0)))
    base = jax.random.normal(jax.random.fold_in(key, 102), (K, FEATURE_DIM), jnp.float32)
    return (base, col_scale)


def row_scales(key, count):
    return jnp.exp(jax.random.uniform(key, (count,), jnp.float32, 0.0, math.log(10.0)))


def draw_centroids(key, part):
    base, col_scale = shared_parts(key)
    noise = jax.random.normal(jax.random.fold_in(key, 103), (K, FEATURE_DIM), jnp.float32)
    scaled = (base + noise) * col_scale[None, :] * row_scales(jax.random.fold_in(key, 104), K)[:, None]
    return jnp.clip(scaled, -400.0, 400.0).astype(jnp.bfloat16)


def draw_embeddings(key, part):
    base, col_scale = shared_parts(key)
    labels = jax.random.randint(jax.random.fold_in(key, 105), (N,), 0, K)
    picked = base[labels]
    picked = picked + jax.random.normal(jax.random.fold_in(key, 106), (N, FEATURE_DIM), jnp.float32)
    scaled = picked * col_scale[None, :] * row_scales(jax.random.fold_in(key, 108), N)[:, None]
    return jnp.clip(scaled, -400.0, 400.0).astype(jnp.bfloat16)


def setup_inputs(seed: int = 0) -> dict:
    key_list = jax.random.split(jax.random.key(seed), 3)
    return {
        "embeddings": draw_embeddings(jax.random.fold_in(key_list[2], 71), 0),
        "centroids": draw_centroids(jax.random.fold_in(key_list[2], 71), 0),
    }


entropy_regularizer = 0.05

def normalize(values):
    wide = values.astype(jnp.float32)
    meansq = lax.optimization_barrier(jnp.mean(wide * wide, axis=-1, keepdims=True))
    return (wide * lax.rsqrt(meansq + 1e-06)).astype(jnp.bfloat16)

def reference(embeddings, centroids):
    normed = normalize(embeddings)
    cent_normed = normalize(centroids)
    sharpness_coefficient = 1.0 / (FEATURE_DIM * entropy_regularizer)
    row_extent = math.gcd(N, 1024)
    blocks = normed.reshape(N // row_extent, row_extent, FEATURE_DIM)
    balance_ratio = N / K

    def kernel_of(row_block):
        cosine_matches = jnp.dot(row_block, cent_normed.T, preferred_element_type=jnp.float32)
        return jnp.exp(cosine_matches * sharpness_coefficient)
    column_factor = jnp.ones((K,), jnp.float32)
    for sweep in range(ROUNDS):

        def step_forward(running, row_block):
            boltzmann_affinity = kernel_of(row_block)
            row_weight = 1.0 / jnp.dot(boltzmann_affinity, column_factor, precision=lax.Precision.HIGHEST)
            return (running + jnp.dot(row_weight, boltzmann_affinity, precision=lax.Precision.HIGHEST), None)
        col_totals, unused = lax.scan(step_forward, jnp.zeros((K,), jnp.float32), blocks)
        column_factor = balance_ratio / col_totals

    def complete_pass(carry, row_block):
        weighted, col_mass = carry
        boltzmann_affinity = kernel_of(row_block)
        row_weight = 1.0 / jnp.dot(boltzmann_affinity, column_factor, precision=lax.Precision.HIGHEST)
        transport = (row_weight[:, None] * boltzmann_affinity * column_factor[None, :]).astype(jnp.bfloat16)
        weighted = weighted + jnp.dot(transport.T, row_block, preferred_element_type=jnp.float32)
        col_mass = col_mass + lax.optimization_barrier(jnp.sum(transport, axis=0, dtype=jnp.float32))
        return ((weighted, col_mass), None)
    start_carry = (jnp.zeros((K, FEATURE_DIM), jnp.float32), jnp.zeros((K,), jnp.float32))
    (weighted, col_mass), unused = lax.scan(complete_pass, start_carry, blocks)
    return weighted / col_mass[:, None]
```

```python
import jax
import jax.numpy as jnp
import numpy as np
from jax import lax
from jax.sharding import Mesh, PartitionSpec as P

FEATURE_DIM = 768
ROUNDS = 2


entropy_regularizer = 0.05


def normalize(values):
    wide = values.astype(jnp.float32)
    meansq = jnp.mean(wide * wide, axis=-1, keepdims=True)
    return (wide * lax.rsqrt(meansq + 1e-06)).astype(jnp.bfloat16)


def cent_sum(x):
    return lax.psum(lax.psum(x, "core"), "cx")


def dp_sum(x):
    return lax.psum(lax.psum(x, "dz"), "dy")


def dp_scatter(x, ny, nz):
    rows = x.shape[0] // (ny * nz)
    rest = x.shape[1:]
    x = x.reshape((ny, nz, rows) + rest)
    x = jnp.swapaxes(x, 0, 1).reshape((nz * ny * rows,) + rest)
    x = lax.psum_scatter(x, "dz", scatter_dimension=0, tiled=True)
    return lax.psum_scatter(x, "dy", scatter_dimension=0, tiled=True)


def row_update(boltzmann_affinity, column_factor):
    partial_rows = jnp.dot(boltzmann_affinity, column_factor, precision=lax.Precision.HIGHEST)
    return 1.0 / cent_sum(partial_rows)


def shards(embeddings, centroids):
    ny = lax.axis_size("dy")
    nz = lax.axis_size("dz")
    normed = normalize(embeddings)
    cent_normed = normalize(centroids)
    cosine_matches = lax.dot_general(
        normed, cent_normed, (((1,), (1,)), ((), ())), preferred_element_type=jnp.float32
    )
    boltzmann_affinity = jnp.exp(cosine_matches * (1.0 / (FEATURE_DIM * entropy_regularizer)))
    local_cents = centroids.shape[0]
    row_count = embeddings.shape[0] * ny * nz
    cent_count = local_cents * lax.axis_size("cx") * lax.axis_size("core")
    balance_ratio = row_count / cent_count
    column_factor = jnp.ones((local_cents,), jnp.float32)
    for sweep in range(ROUNDS):
        row_weight = row_update(boltzmann_affinity, column_factor)
        partial_cols = jnp.dot(row_weight, boltzmann_affinity, precision=lax.Precision.HIGHEST)
        column_factor = balance_ratio / dp_sum(partial_cols)
    row_weight = row_update(boltzmann_affinity, column_factor)
    transport = (row_weight[:, None] * boltzmann_affinity * column_factor[None, :]).astype(
        jnp.bfloat16
    )
    col_mass = jnp.sum(transport, axis=0, dtype=jnp.float32)
    col_mass = dp_scatter(col_mass, ny, nz)
    weighted = lax.dot_general(
        transport, normed, (((0,), (0,)), ((), ())), preferred_element_type=jnp.float32
    )
    weighted = dp_scatter(weighted, ny, nz)
    return weighted / col_mass[:, None]


def split_mesh(mesh):
    devices = mesh.devices
    n_dp, n_cent = devices.shape
    try:
        ny = len({d.coords[1] for d in devices.flat})
        ncore = len({d.core_on_chip for d in devices.flat})
    except AttributeError:
        ny, ncore = 4, 2
    return Mesh(
        devices.reshape(ny, n_dp // ny, n_cent // ncore, ncore), ("dy", "dz", "cx", "core")
    )


def solution(mesh):
    sub = split_mesh(mesh)
    in_specs = (P(("dy", "dz"), None), P(("cx", "core"), None))
    out_specs = P(("cx", "core", "dy", "dz"), None)
    return jax.shard_map(shards, mesh=sub, in_specs=in_specs, out_specs=out_specs, check_vma=False)
```

```python
import jax
import jax.numpy as jnp
import numpy as np
from jax import lax
from jax.sharding import Mesh, PartitionSpec as P

FEATURE_DIM = 768
ROUNDS = 2


entropy_regularizer = 0.05


def normalize_wide(values):
    wide = values.astype(jnp.float32)
    meansq = jnp.mean(wide * wide, axis=-1, keepdims=True)
    return wide * lax.rsqrt(meansq + 1e-06)


def normalize(values):
    return normalize_wide(values).astype(jnp.bfloat16)


def cent_sum(x):
    return lax.psum(lax.psum(x, "core"), "cx")


def dp_sum(x):
    return lax.psum(lax.psum(x, "dz"), "dy")


def row_update(boltzmann_affinity, column_factor):
    partial_rows = jnp.dot(boltzmann_affinity, column_factor, precision=lax.Precision.HIGHEST)
    return 1.0 / cent_sum(partial_rows)


def shards(embeddings, centroids):
    ny = lax.axis_size("dy")
    nz = lax.axis_size("dz")
    scaled_rows = normalize_wide(embeddings)
    normed = scaled_rows.astype(jnp.bfloat16)
    cent_normed = normalize(centroids)
    cosine_matches = lax.dot_general(
        normed, cent_normed, (((1,), (1,)), ((), ())), preferred_element_type=jnp.float32
    )
    boltzmann_affinity = jnp.exp(cosine_matches * (1.0 / (FEATURE_DIM * entropy_regularizer)))
    local_cents = centroids.shape[0]
    row_count = embeddings.shape[0] * ny * nz
    cent_count = local_cents * lax.axis_size("cx") * lax.axis_size("core")
    balance_ratio = row_count / cent_count
    column_factor = jnp.ones((local_cents,), jnp.float32)
    for sweep in range(ROUNDS):
        row_weight = row_update(boltzmann_affinity, column_factor)
        partial_cols = jnp.dot(row_weight, boltzmann_affinity, precision=lax.Precision.HIGHEST)
        column_factor = balance_ratio / dp_sum(partial_cols)
    row_weight = row_update(boltzmann_affinity, column_factor)
    gathered = lax.all_gather(scaled_rows, "dy", axis=0, tiled=True)
    unit = column_factor[0] * 0.0 + 1.0
    gathered = (gathered * unit).astype(jnp.bfloat16)
    gathered_weight = lax.all_gather(row_weight, "dy", axis=0, tiled=True)
    sub_cents = local_cents // ny
    start = lax.axis_index("dy") * sub_cents
    sub_normed = lax.dynamic_slice_in_dim(cent_normed, start, sub_cents, 0)
    sub_factor = lax.dynamic_slice_in_dim(column_factor, start, sub_cents, 0)
    sub_matches = lax.dot_general(
        gathered, sub_normed, (((1,), (1,)), ((), ())), preferred_element_type=jnp.float32
    )
    sub_affinity = jnp.exp(sub_matches * (1.0 / (FEATURE_DIM * entropy_regularizer)))
    transport = (gathered_weight[:, None] * sub_affinity * sub_factor[None, :]).astype(
        jnp.bfloat16
    )
    col_mass = jnp.sum(transport, axis=0, dtype=jnp.float32)
    weighted = lax.dot_general(
        transport, gathered, (((0,), (0,)), ((), ())), preferred_element_type=jnp.float32
    )
    weighted, col_mass = lax.psum_scatter(
        (weighted, col_mass), "dz", scatter_dimension=0, tiled=True
    )
    return weighted / col_mass[:, None]


def split_mesh(mesh):
    devices = mesh.devices
    n_dp, n_cent = devices.shape
    try:
        ny = len({d.coords[1] for d in devices.flat})
        ncore = len({d.core_on_chip for d in devices.flat})
    except AttributeError:
        ny, ncore = 4, 2
    return Mesh(
        devices.reshape(ny, n_dp // ny, n_cent // ncore, ncore), ("dy", "dz", "cx", "core")
    )


def solution(mesh):
    sub = split_mesh(mesh)
    in_specs = (P(("dy", "dz"), None), P(("cx", "core"), None))
    out_specs = P(("cx", "core", "dy", "dz"), None)
    return jax.shard_map(shards, mesh=sub, in_specs=in_specs, out_specs=out_specs, check_vma=False)
```

```python
import jax
import jax.numpy as jnp
import numpy as np
from jax import lax
from jax.sharding import Mesh, PartitionSpec as P

FEATURE_DIM = 768
ROUNDS = 2


entropy_regularizer = 0.05


def normalize_wide(values):
    wide = values.astype(jnp.float32)
    meansq = jnp.mean(wide * wide, axis=-1, keepdims=True)
    return wide * lax.rsqrt(meansq + 1e-06)


def normalize(values):
    return normalize_wide(values).astype(jnp.bfloat16)


def cent_sum(x):
    return lax.psum(lax.psum(x, "core"), "cx")


def dp_sum(x):
    return lax.psum(lax.psum(x, "dz"), "dy")


def row_update(boltzmann_affinity, column_factor):
    partial_rows = jnp.sum(boltzmann_affinity * column_factor[None, :], axis=1)
    return 1.0 / cent_sum(partial_rows)


def shards(embeddings, centroids):
    ny = lax.axis_size("dy")
    nz = lax.axis_size("dz")
    scaled_rows = normalize_wide(embeddings)
    normed = scaled_rows.astype(jnp.bfloat16)
    cent_normed = normalize(centroids)
    cosine_matches = lax.dot_general(
        normed, cent_normed, (((1,), (1,)), ((), ())), preferred_element_type=jnp.float32
    )
    boltzmann_affinity = jnp.exp(cosine_matches * (1.0 / (FEATURE_DIM * entropy_regularizer)))
    local_cents = centroids.shape[0]
    row_count = embeddings.shape[0] * ny * nz
    cent_count = local_cents * lax.axis_size("cx") * lax.axis_size("core")
    balance_ratio = row_count / cent_count
    column_factor = jnp.ones((local_cents,), jnp.float32)
    for sweep in range(ROUNDS):
        row_weight = row_update(boltzmann_affinity, column_factor)
        partial_cols = jnp.sum(row_weight[:, None] * boltzmann_affinity, axis=0)
        column_factor = balance_ratio / dp_sum(partial_cols)
    row_weight = row_update(boltzmann_affinity, column_factor)
    gathered = lax.all_gather(scaled_rows, "dy", axis=0, tiled=True)
    unit = column_factor[0] * 0.0 + 1.0
    gathered = (gathered * unit).astype(jnp.bfloat16)
    gathered_weight = lax.all_gather(row_weight, "dy", axis=0, tiled=True)
    sub_cents = local_cents // ny
    start = lax.axis_index("dy") * sub_cents
    sub_normed = lax.dynamic_slice_in_dim(cent_normed, start, sub_cents, 0)
    sub_factor = lax.dynamic_slice_in_dim(column_factor, start, sub_cents, 0)
    sub_matches = lax.dot_general(
        gathered, sub_normed, (((1,), (1,)), ((), ())), preferred_element_type=jnp.float32
    )
    sub_affinity = jnp.exp(sub_matches * (1.0 / (FEATURE_DIM * entropy_regularizer)))
    transport = (gathered_weight[:, None] * sub_affinity * sub_factor[None, :]).astype(
        jnp.bfloat16
    )
    col_mass = jnp.sum(transport, axis=0, dtype=jnp.float32)
    weighted = lax.dot_general(
        transport, gathered, (((0,), (0,)), ((), ())), preferred_element_type=jnp.float32
    )
    weighted, col_mass = lax.psum_scatter(
        (weighted, col_mass), "dz", scatter_dimension=0, tiled=True
    )
    return weighted / col_mass[:, None]


def split_mesh(mesh):
    devices = mesh.devices
    n_dp, n_cent = devices.shape
    try:
        ny = len({d.coords[1] for d in devices.flat})
        ncore = len({d.core_on_chip for d in devices.flat})
    except AttributeError:
        ny, ncore = 4, 2
    return Mesh(
        devices.reshape(ny, n_dp // ny, n_cent // ncore, ncore), ("dy", "dz", "cx", "core")
    )


def solution(mesh):
    sub = split_mesh(mesh)
    in_specs = (P(("dy", "dz"), None), P(("cx", "core"), None))
    out_specs = P(("cx", "core", "dy", "dz"), None)
    return jax.shard_map(shards, mesh=sub, in_specs=in_specs, out_specs=out_specs, check_vma=False)
```

```python
import jax
import jax.numpy as jnp
import numpy as np
from jax import lax
from jax.sharding import Mesh, PartitionSpec as P

FEATURE_DIM = 768
ROUNDS = 2


entropy_regularizer = 0.05


def normalize_wide(values):
    wide = values.astype(jnp.float32)
    meansq = jnp.mean(wide * wide, axis=-1, keepdims=True)
    return wide * lax.rsqrt(meansq + 1e-06)


def normalize(values):
    return normalize_wide(values).astype(jnp.bfloat16)


def cent_sum(x):
    return lax.psum(lax.psum(x, "core"), "cx")


def dp_sum(x):
    return lax.psum(lax.psum(x, "dz"), "dy")


def row_update(boltzmann_affinity, column_factor):
    partial_rows = jnp.sum(boltzmann_affinity * column_factor[None, :], axis=1)
    return 1.0 / cent_sum(partial_rows)


def shards(embeddings, centroids):
    ny = lax.axis_size("dy")
    nz = lax.axis_size("dz")
    scaled_rows = normalize_wide(embeddings)
    normed = scaled_rows.astype(jnp.bfloat16)
    cent_normed = normalize(centroids)
    cosine_matches = lax.dot_general(
        normed, cent_normed, (((1,), (1,)), ((), ())), preferred_element_type=jnp.float32
    )
    boltzmann_affinity = jnp.exp(cosine_matches * (1.0 / (FEATURE_DIM * entropy_regularizer)))
    local_cents = centroids.shape[0]
    row_count = embeddings.shape[0] * ny * nz
    cent_count = local_cents * lax.axis_size("cx") * lax.axis_size("core")
    balance_ratio = row_count / cent_count
    column_factor = jnp.ones((local_cents,), jnp.float32)
    for sweep in range(ROUNDS):
        row_weight = row_update(boltzmann_affinity, column_factor)
        partial_cols = jnp.sum(row_weight[:, None] * boltzmann_affinity, axis=0)
        column_factor = balance_ratio / dp_sum(partial_cols)
    scaled_all = lax.all_gather(scaled_rows, "dy", axis=0, tiled=True)
    unit = scaled_rows[0, 0] * 0.0 + 1.0
    gathered = (scaled_all * unit).astype(jnp.bfloat16)
    sub_cents = local_cents // ny
    start = lax.axis_index("dy") * sub_cents
    sub_normed = lax.dynamic_slice_in_dim(cent_normed, start, sub_cents, 0)
    sub_factor = lax.dynamic_slice_in_dim(column_factor, start, sub_cents, 0)
    sub_matches = lax.dot_general(
        gathered, sub_normed, (((1,), (1,)), ((), ())), preferred_element_type=jnp.float32
    )
    sub_affinity = jnp.exp(sub_matches * (1.0 / (FEATURE_DIM * entropy_regularizer)))
    sub_rows = jnp.sum(sub_affinity * sub_factor[None, :], axis=1)
    gathered_weight = 1.0 / lax.psum(cent_sum(sub_rows), "dy")
    transport = (gathered_weight[:, None] * sub_affinity * sub_factor[None, :]).astype(
        jnp.bfloat16
    )
    col_mass = jnp.sum(transport, axis=0, dtype=jnp.float32)
    weighted = lax.dot_general(
        transport, gathered, (((0,), (0,)), ((), ())), preferred_element_type=jnp.float32
    )
    weighted, col_mass = lax.psum_scatter(
        (weighted, col_mass), "dz", scatter_dimension=0, tiled=True
    )
    return weighted / col_mass[:, None]


def split_mesh(mesh):
    devices = mesh.devices
    n_dp, n_cent = devices.shape
    try:
        ny = len({d.coords[1] for d in devices.flat})
        ncore = len({d.core_on_chip for d in devices.flat})
    except AttributeError:
        ny, ncore = 4, 2
    return Mesh(
        devices.reshape(ny, n_dp // ny, n_cent // ncore, ncore), ("dy", "dz", "cx", "core")
    )


def solution(mesh):
    sub = split_mesh(mesh)
    in_specs = (P(("dy", "dz"), None), P(("cx", "core"), None))
    out_specs = P(("cx", "core", "dy", "dz"), None)
    return jax.shard_map(shards, mesh=sub, in_specs=in_specs, out_specs=out_specs, check_vma=False)
```

```python
import jax
import jax.numpy as jnp
import numpy as np
from jax import lax
from jax.sharding import Mesh, PartitionSpec as P

FEATURE_DIM = 768
ROUNDS = 2


entropy_regularizer = 0.05


def normalize_wide(values):
    wide = values.astype(jnp.float32)
    meansq = jnp.mean(wide * wide, axis=-1, keepdims=True)
    return wide * lax.rsqrt(meansq + 1e-06)


def normalize(values):
    return normalize_wide(values).astype(jnp.bfloat16)


def cent_sum(x):
    n = lax.axis_size("cx") * lax.axis_size("core")
    step = 1
    while step < n:
        pairs = [(i, i ^ step) for i in range(n)]
        x = x + lax.ppermute(x, ("cx", "core"), pairs)
        step *= 2
    return x


def dp_sum(x):
    return lax.psum(lax.psum(x, "dz"), "dy")


def row_update(boltzmann_affinity, column_factor):
    partial_rows = jnp.sum(boltzmann_affinity * column_factor[None, :], axis=1)
    return 1.0 / cent_sum(partial_rows)


def shards(embeddings, centroids):
    ny = lax.axis_size("dy")
    nz = lax.axis_size("dz")
    scaled_rows = normalize_wide(embeddings)
    normed = scaled_rows.astype(jnp.bfloat16)
    cent_normed = normalize(centroids)
    cosine_matches = lax.dot_general(
        normed, cent_normed, (((1,), (1,)), ((), ())), preferred_element_type=jnp.float32
    )
    boltzmann_affinity = jnp.exp(cosine_matches * (1.0 / (FEATURE_DIM * entropy_regularizer)))
    local_cents = centroids.shape[0]
    row_count = embeddings.shape[0] * ny * nz
    cent_count = local_cents * lax.axis_size("cx") * lax.axis_size("core")
    balance_ratio = row_count / cent_count
    column_factor = jnp.ones((local_cents,), jnp.float32)
    for sweep in range(ROUNDS):
        row_weight = row_update(boltzmann_affinity, column_factor)
        partial_cols = jnp.sum(row_weight[:, None] * boltzmann_affinity, axis=0)
        column_factor = balance_ratio / dp_sum(partial_cols)
    row_weight = row_update(boltzmann_affinity, column_factor)
    gathered = lax.all_gather(scaled_rows, "dy", axis=0, tiled=True)
    unit = column_factor[0] * 0.0 + 1.0
    gathered = (gathered * unit).astype(jnp.bfloat16)
    gathered_weight = lax.all_gather(row_weight, "dy", axis=0, tiled=True)
    sub_cents = local_cents // ny
    start = lax.axis_index("dy") * sub_cents
    sub_normed = lax.dynamic_slice_in_dim(cent_normed, start, sub_cents, 0)
    sub_factor = lax.dynamic_slice_in_dim(column_factor, start, sub_cents, 0)
    sub_matches = lax.dot_general(
        gathered, sub_normed, (((1,), (1,)), ((), ())), preferred_element_type=jnp.float32
    )
    sub_affinity = jnp.exp(sub_matches * (1.0 / (FEATURE_DIM * entropy_regularizer)))
    transport = (gathered_weight[:, None] * sub_affinity * sub_factor[None, :]).astype(
        jnp.bfloat16
    )
    col_mass = jnp.sum(transport, axis=0, dtype=jnp.float32)
    weighted = lax.dot_general(
        transport, gathered, (((0,), (0,)), ((), ())), preferred_element_type=jnp.float32
    )
    weighted, col_mass = lax.psum_scatter(
        (weighted, col_mass), "dz", scatter_dimension=0, tiled=True
    )
    return weighted / col_mass[:, None]


def split_mesh(mesh):
    devices = mesh.devices
    n_dp, n_cent = devices.shape
    try:
        ny = len({d.coords[1] for d in devices.flat})
        ncore = len({d.core_on_chip for d in devices.flat})
    except AttributeError:
        ny, ncore = 4, 2
    return Mesh(
        devices.reshape(ny, n_dp // ny, n_cent // ncore, ncore), ("dy", "dz", "cx", "core")
    )


def solution(mesh):
    sub = split_mesh(mesh)
    in_specs = (P(("dy", "dz"), None), P(("cx", "core"), None))
    out_specs = P(("cx", "core", "dy", "dz"), None)
    return jax.shard_map(shards, mesh=sub, in_specs=in_specs, out_specs=out_specs, check_vma=False)
```

```python
import jax
import jax.numpy as jnp
import numpy as np
from jax import lax
from jax.sharding import Mesh, PartitionSpec as P

FEATURE_DIM = 768
ROUNDS = 2


entropy_regularizer = 0.05


def normalize_wide(values):
    wide = values.astype(jnp.float32)
    meansq = jnp.mean(wide * wide, axis=-1, keepdims=True)
    return wide * lax.rsqrt(meansq + 1e-06)


def normalize(values):
    return normalize_wide(values).astype(jnp.bfloat16)


def doubling_sum(x, axes):
    n = 1
    for a in axes:
        n *= lax.axis_size(a)
    step = 1
    while step < n:
        pairs = [(i, i ^ step) for i in range(n)]
        x = x + lax.ppermute(x, axes, pairs)
        step *= 2
    return x


def cent_sum(x):
    return doubling_sum(x, ("cx", "core"))


def dp_sum(x):
    return doubling_sum(x, ("dy", "dz"))


def doubling_gather(x, axis):
    n = lax.axis_size(axis)
    slots = jnp.zeros((n,) + x.shape, x.dtype)
    slots = lax.dynamic_update_index_in_dim(slots, x, lax.axis_index(axis), 0)
    return doubling_sum(slots, (axis,)).reshape((n * x.shape[0],) + x.shape[1:])


def row_update(boltzmann_affinity, column_factor):
    partial_rows = jnp.sum(boltzmann_affinity * column_factor[None, :], axis=1)
    return 1.0 / cent_sum(partial_rows)


def shards(embeddings, centroids):
    ny = lax.axis_size("dy")
    nz = lax.axis_size("dz")
    scaled_rows = normalize_wide(embeddings)
    normed = scaled_rows.astype(jnp.bfloat16)
    cent_normed = normalize(centroids)
    cosine_matches = lax.dot_general(
        normed, cent_normed, (((1,), (1,)), ((), ())), preferred_element_type=jnp.float32
    )
    boltzmann_affinity = jnp.exp(cosine_matches * (1.0 / (FEATURE_DIM * entropy_regularizer)))
    local_cents = centroids.shape[0]
    row_count = embeddings.shape[0] * ny * nz
    cent_count = local_cents * lax.axis_size("cx") * lax.axis_size("core")
    balance_ratio = row_count / cent_count
    column_factor = jnp.ones((local_cents,), jnp.float32)
    for sweep in range(ROUNDS):
        row_weight = row_update(boltzmann_affinity, column_factor)
        partial_cols = jnp.sum(row_weight[:, None] * boltzmann_affinity, axis=0)
        column_factor = balance_ratio / dp_sum(partial_cols)
    row_weight = row_update(boltzmann_affinity, column_factor)
    gathered = lax.all_gather(scaled_rows, "dy", axis=0, tiled=True)
    unit = column_factor[0] * 0.0 + 1.0
    gathered = (gathered * unit).astype(jnp.bfloat16)
    gathered_weight = doubling_gather(row_weight, "dy")
    sub_cents = local_cents // ny
    start = lax.axis_index("dy") * sub_cents
    sub_normed = lax.dynamic_slice_in_dim(cent_normed, start, sub_cents, 0)
    sub_factor = lax.dynamic_slice_in_dim(column_factor, start, sub_cents, 0)
    sub_matches = lax.dot_general(
        gathered, sub_normed, (((1,), (1,)), ((), ())), preferred_element_type=jnp.float32
    )
    sub_affinity = jnp.exp(sub_matches * (1.0 / (FEATURE_DIM * entropy_regularizer)))
    transport = (gathered_weight[:, None] * sub_affinity * sub_factor[None, :]).astype(
        jnp.bfloat16
    )
    col_mass = jnp.sum(transport, axis=0, dtype=jnp.float32)
    weighted = lax.dot_general(
        transport, gathered, (((0,), (0,)), ((), ())), preferred_element_type=jnp.float32
    )
    weighted, col_mass = lax.psum_scatter(
        (weighted, col_mass), "dz", scatter_dimension=0, tiled=True
    )
    return weighted / col_mass[:, None]


def split_mesh(mesh):
    devices = mesh.devices
    n_dp, n_cent = devices.shape
    try:
        ny = len({d.coords[1] for d in devices.flat})
        ncore = len({d.core_on_chip for d in devices.flat})
    except AttributeError:
        ny, ncore = 4, 2
    return Mesh(
        devices.reshape(ny, n_dp // ny, n_cent // ncore, ncore), ("dy", "dz", "cx", "core")
    )


def solution(mesh):
    sub = split_mesh(mesh)
    in_specs = (P(("dy", "dz"), None), P(("cx", "core"), None))
    out_specs = P(("cx", "core", "dy", "dz"), None)
    return jax.shard_map(shards, mesh=sub, in_specs=in_specs, out_specs=out_specs, check_vma=False)
```

```python
import jax
import jax.numpy as jnp
import numpy as np
from jax import lax
from jax.sharding import Mesh, PartitionSpec as P

FEATURE_DIM = 768
ROUNDS = 2


entropy_regularizer = 0.05


def normalize_wide(values):
    wide = values.astype(jnp.float32)
    meansq = jnp.mean(wide * wide, axis=-1, keepdims=True)
    return wide * lax.rsqrt(meansq + 1e-06)


def normalize(values):
    return normalize_wide(values).astype(jnp.bfloat16)


def doubling_sum(x, axes):
    n = 1
    for a in axes:
        n *= lax.axis_size(a)
    step = 1
    while step < n:
        pairs = [(i, i ^ step) for i in range(n)]
        x = x + lax.ppermute(x, axes, pairs)
        step *= 2
    return x


def cent_sum(x):
    return doubling_sum(x, ("cx", "core"))


def dp_sum(x):
    return doubling_sum(x, ("dy", "dz"))


def doubling_gather(x, axis):
    n = lax.axis_size(axis)
    slots = jnp.zeros((n,) + x.shape, x.dtype)
    slots = lax.dynamic_update_index_in_dim(slots, x, lax.axis_index(axis), 0)
    return doubling_sum(slots, (axis,)).reshape((n * x.shape[0],) + x.shape[1:])


def row_update(boltzmann_affinity, column_factor):
    partial_rows = jnp.sum(boltzmann_affinity * column_factor[None, :], axis=1)
    return 1.0 / cent_sum(partial_rows)


def shards(embeddings, centroids):
    ny = lax.axis_size("dy")
    nz = lax.axis_size("dz")
    scaled_rows = normalize_wide(embeddings)
    normed = scaled_rows.astype(jnp.bfloat16)
    cent_normed = normalize(centroids)
    cosine_matches = lax.dot_general(
        normed, cent_normed, (((1,), (1,)), ((), ())), preferred_element_type=jnp.float32
    )
    boltzmann_affinity = jnp.exp(cosine_matches * (1.0 / (FEATURE_DIM * entropy_regularizer)))
    local_cents = centroids.shape[0]
    row_count = embeddings.shape[0] * ny * nz
    cent_count = local_cents * lax.axis_size("cx") * lax.axis_size("core")
    balance_ratio = row_count / cent_count
    column_factor = jnp.ones((local_cents,), jnp.float32)
    for sweep in range(ROUNDS):
        row_weight = row_update(boltzmann_affinity, column_factor)
        partial_cols = jnp.sum(row_weight[:, None] * boltzmann_affinity, axis=0)
        column_factor = balance_ratio / dp_sum(partial_cols)
    row_weight = row_update(boltzmann_affinity, column_factor)
    gathered = lax.all_gather(scaled_rows, "dy", axis=0, tiled=True)
    unit = column_factor[0] * 0.0 + 1.0
    gathered = (gathered * unit).astype(jnp.bfloat16)
    gathered_weight = doubling_gather(row_weight, "dy")
    sub_cents = local_cents // ny
    start = lax.axis_index("dy") * sub_cents
    sub_normed = lax.dynamic_slice_in_dim(cent_normed, start, sub_cents, 0)
    sub_factor = lax.dynamic_slice_in_dim(column_factor, start, sub_cents, 0)
    sub_matches = lax.dot_general(
        gathered, sub_normed, (((1,), (1,)), ((), ())), preferred_element_type=jnp.float32
    )
    sub_affinity = jnp.exp(sub_matches * (1.0 / (FEATURE_DIM * entropy_regularizer)))
    transport = (gathered_weight[:, None] * sub_affinity * sub_factor[None, :]).astype(
        jnp.bfloat16
    )
    col_mass = jnp.sum(transport, axis=0, dtype=jnp.float32)
    weighted = lax.dot_general(
        transport, gathered, (((0,), (0,)), ((), ())), preferred_element_type=jnp.float32
    )
    weighted = lax.psum_scatter(weighted, "dz", scatter_dimension=0, tiled=True)
    own = weighted.shape[0]
    col_mass = lax.dynamic_slice_in_dim(
        doubling_sum(col_mass, ("dz",)), lax.axis_index("dz") * own, own, 0
    )
    return weighted / col_mass[:, None]


def split_mesh(mesh):
    devices = mesh.devices
    n_dp, n_cent = devices.shape
    try:
        ny = len({d.coords[1] for d in devices.flat})
        ncore = len({d.core_on_chip for d in devices.flat})
    except AttributeError:
        ny, ncore = 4, 2
    return Mesh(
        devices.reshape(ny, n_dp // ny, n_cent // ncore, ncore), ("dy", "dz", "cx", "core")
    )


def solution(mesh):
    sub = split_mesh(mesh)
    in_specs = (P(("dy", "dz"), None), P(("cx", "core"), None))
    out_specs = P(("cx", "core", "dy", "dz"), None)
    return jax.shard_map(shards, mesh=sub, in_specs=in_specs, out_specs=out_specs, check_vma=False)
```

```python
import jax
import jax.numpy as jnp
import numpy as np
from jax import lax
from jax.sharding import Mesh, PartitionSpec as P

FEATURE_DIM = 768
ROUNDS = 2


entropy_regularizer = 0.05


def normalize_wide(values):
    wide = values.astype(jnp.float32)
    meansq = jnp.mean(wide * wide, axis=-1, keepdims=True)
    return wide * lax.rsqrt(meansq + 1e-06)


def normalize(values):
    return normalize_wide(values).astype(jnp.bfloat16)


def doubling_sum(x, axes):
    for a in axes:
        n = lax.axis_size(a)
        step = 1
        while step < n:
            if 2 * step == n:
                pairs = [(i, n - 1 - i) for i in range(n)]
            else:
                pairs = [(i, i ^ step) for i in range(n)]
            x = x + lax.ppermute(x, a, pairs)
            step *= 2
    return x


def cent_sum(x):
    return doubling_sum(x, ("core", "cx"))


def dp_sum(x):
    return doubling_sum(x, ("dz", "dy"))


def doubling_gather(x, axis):
    n = lax.axis_size(axis)
    slots = jnp.zeros((n,) + x.shape, x.dtype)
    slots = lax.dynamic_update_index_in_dim(slots, x, lax.axis_index(axis), 0)
    return doubling_sum(slots, (axis,)).reshape((n * x.shape[0],) + x.shape[1:])


def row_update(boltzmann_affinity, column_factor):
    partial_rows = jnp.sum(boltzmann_affinity * column_factor[None, :], axis=1)
    return 1.0 / cent_sum(partial_rows)


def shards(embeddings, centroids):
    ny = lax.axis_size("dy")
    nz = lax.axis_size("dz")
    scaled_rows = normalize_wide(embeddings)
    normed = scaled_rows.astype(jnp.bfloat16)
    cent_normed = normalize(centroids)
    cosine_matches = lax.dot_general(
        normed, cent_normed, (((1,), (1,)), ((), ())), preferred_element_type=jnp.float32
    )
    boltzmann_affinity = jnp.exp(cosine_matches * (1.0 / (FEATURE_DIM * entropy_regularizer)))
    local_cents = centroids.shape[0]
    row_count = embeddings.shape[0] * ny * nz
    cent_count = local_cents * lax.axis_size("cx") * lax.axis_size("core")
    balance_ratio = row_count / cent_count
    column_factor = jnp.ones((local_cents,), jnp.float32)
    for sweep in range(ROUNDS):
        row_weight = row_update(boltzmann_affinity, column_factor)
        partial_cols = jnp.sum(row_weight[:, None] * boltzmann_affinity, axis=0)
        column_factor = balance_ratio / dp_sum(partial_cols)
    row_weight = row_update(boltzmann_affinity, column_factor)
    gathered = lax.all_gather(scaled_rows, "dy", axis=0, tiled=True)
    unit = column_factor[0] * 0.0 + 1.0
    gathered = (gathered * unit).astype(jnp.bfloat16)
    gathered_weight = doubling_gather(row_weight, "dy")
    sub_cents = local_cents // ny
    start = lax.axis_index("dy") * sub_cents
    sub_normed = lax.dynamic_slice_in_dim(cent_normed, start, sub_cents, 0)
    sub_factor = lax.dynamic_slice_in_dim(column_factor, start, sub_cents, 0)
    sub_matches = lax.dot_general(
        gathered, sub_normed, (((1,), (1,)), ((), ())), preferred_element_type=jnp.float32
    )
    sub_affinity = jnp.exp(sub_matches * (1.0 / (FEATURE_DIM * entropy_regularizer)))
    transport = (gathered_weight[:, None] * sub_affinity * sub_factor[None, :]).astype(
        jnp.bfloat16
    )
    col_mass = jnp.sum(transport, axis=0, dtype=jnp.float32)
    weighted = lax.dot_general(
        transport, gathered, (((0,), (0,)), ((), ())), preferred_element_type=jnp.float32
    )
    weighted, col_mass = lax.psum_scatter(
        (weighted, col_mass), "dz", scatter_dimension=0, tiled=True
    )
    return weighted / col_mass[:, None]


def split_mesh(mesh):
    devices = mesh.devices
    n_dp, n_cent = devices.shape
    try:
        ny = len({d.coords[1] for d in devices.flat})
        ncore = len({d.core_on_chip for d in devices.flat})
    except AttributeError:
        ny, ncore = 4, 2
    return Mesh(
        devices.reshape(ny, n_dp // ny, n_cent // ncore, ncore), ("dy", "dz", "cx", "core")
    )


def solution(mesh):
    sub = split_mesh(mesh)
    in_specs = (P(("dy", "dz"), None), P(("cx", "core"), None))
    out_specs = P(("cx", "core", "dy", "dz"), None)
    return jax.shard_map(shards, mesh=sub, in_specs=in_specs, out_specs=out_specs, check_vma=False)
```

```python
import jax
import jax.numpy as jnp
import numpy as np
from jax import lax
from jax.sharding import Mesh, PartitionSpec as P

FEATURE_DIM = 768
ROUNDS = 2


entropy_regularizer = 0.05


def normalize_wide(values):
    wide = values.astype(jnp.float32)
    meansq = jnp.mean(wide * wide, axis=-1, keepdims=True)
    return wide * lax.rsqrt(meansq + 1e-06)


def normalize(values):
    return normalize_wide(values).astype(jnp.bfloat16)


def doubling_sum(x, axes):
    for a in axes:
        n = lax.axis_size(a)
        step = 1
        while step < n:
            if 2 * step == n:
                pairs = [(i, n - 1 - i) for i in range(n)]
            else:
                pairs = [(i, i ^ step) for i in range(n)]
            x = x + lax.ppermute(x, a, pairs)
            step *= 2
    return x


def cent_sum(x):
    return doubling_sum(x, ("core", "cx"))


def dp_sum(x):
    return doubling_sum(x, ("dz", "dy"))


def doubling_gather(x, axis):
    n = lax.axis_size(axis)
    slots = jnp.zeros((n,) + x.shape, x.dtype)
    slots = lax.dynamic_update_index_in_dim(slots, x, lax.axis_index(axis), 0)
    return doubling_sum(slots, (axis,)).reshape((n * x.shape[0],) + x.shape[1:])


def ring_gather(x, axis):
    n = lax.axis_size(axis)
    blocks = [x]
    for k in range(1, n):
        blocks.append(lax.ppermute(x, axis, [(i, (i + k) % n) for i in range(n)]))
    return jnp.concatenate(blocks, axis=0)


def exchange_sum(x, axis):
    n = lax.axis_size(axis)
    parts = x.reshape((n, x.shape[0] // n) + x.shape[1:])
    return jnp.sum(lax.all_to_all(parts, axis, 0, 0, tiled=False), axis=0)


def row_update(boltzmann_affinity, column_factor):
    partial_rows = jnp.sum(boltzmann_affinity * column_factor[None, :], axis=1)
    return 1.0 / cent_sum(partial_rows)


def shards(embeddings, centroids):
    ny = lax.axis_size("dy")
    nz = lax.axis_size("dz")
    scaled_rows = normalize_wide(embeddings)
    normed = scaled_rows.astype(jnp.bfloat16)
    cent_normed = normalize(centroids)
    cosine_matches = lax.dot_general(
        normed, cent_normed, (((1,), (1,)), ((), ())), preferred_element_type=jnp.float32
    )
    boltzmann_affinity = jnp.exp(cosine_matches * (1.0 / (FEATURE_DIM * entropy_regularizer)))
    local_cents = centroids.shape[0]
    row_count = embeddings.shape[0] * ny * nz
    cent_count = local_cents * lax.axis_size("cx") * lax.axis_size("core")
    balance_ratio = row_count / cent_count
    column_factor = jnp.ones((local_cents,), jnp.float32)
    for sweep in range(ROUNDS):
        row_weight = row_update(boltzmann_affinity, column_factor)
        partial_cols = jnp.sum(row_weight[:, None] * boltzmann_affinity, axis=0)
        column_factor = balance_ratio / dp_sum(partial_cols)
    row_weight = row_update(boltzmann_affinity, column_factor)
    gathered = ring_gather(scaled_rows, "dy")
    unit = column_factor[0] * 0.0 + 1.0
    gathered = (gathered * unit).astype(jnp.bfloat16)
    gathered_weight = ring_gather(row_weight, "dy")
    sub_cents = local_cents // ny
    start = lax.axis_index("dy") * sub_cents
    sub_normed = lax.dynamic_slice_in_dim(cent_normed, start, sub_cents, 0)
    sub_factor = lax.dynamic_slice_in_dim(column_factor, start, sub_cents, 0)
    sub_matches = lax.dot_general(
        gathered, sub_normed, (((1,), (1,)), ((), ())), preferred_element_type=jnp.float32
    )
    sub_affinity = jnp.exp(sub_matches * (1.0 / (FEATURE_DIM * entropy_regularizer)))
    transport = (gathered_weight[:, None] * sub_affinity * sub_factor[None, :]).astype(
        jnp.bfloat16
    )
    col_mass = jnp.sum(transport, axis=0, dtype=jnp.float32)
    weighted = lax.dot_general(
        transport, gathered, (((0,), (0,)), ((), ())), preferred_element_type=jnp.float32
    )
    weighted = exchange_sum(weighted, "dz")
    col_mass = exchange_sum(col_mass, "dz")
    return weighted / col_mass[:, None]


def split_mesh(mesh):
    devices = mesh.devices
    n_dp, n_cent = devices.shape
    try:
        ny = len({d.coords[1] for d in devices.flat})
        ncore = len({d.core_on_chip for d in devices.flat})
    except AttributeError:
        ny, ncore = 4, 2
    return Mesh(
        devices.reshape(ny, n_dp // ny, n_cent // ncore, ncore), ("dy", "dz", "cx", "core")
    )


def solution(mesh):
    sub = split_mesh(mesh)
    in_specs = (P(("dy", "dz"), None), P(("cx", "core"), None))
    out_specs = P(("cx", "core", "dy", "dz"), None)
    return jax.shard_map(shards, mesh=sub, in_specs=in_specs, out_specs=out_specs, check_vma=False)
```

```python
import jax
import jax.numpy as jnp
import numpy as np
from jax import lax
from jax.sharding import Mesh, PartitionSpec as P

FEATURE_DIM = 768
ROUNDS = 2


entropy_regularizer = 0.05


def normalize_wide(values):
    wide = values.astype(jnp.float32)
    meansq = jnp.mean(wide * wide, axis=-1, keepdims=True)
    return wide * lax.rsqrt(meansq + 1e-06)


def normalize(values):
    return normalize_wide(values).astype(jnp.bfloat16)


def doubling_sum(x, axes):
    for a in axes:
        n = lax.axis_size(a)
        step = 1
        while step < n:
            if 2 * step == n:
                pairs = [(i, n - 1 - i) for i in range(n)]
            else:
                pairs = [(i, i ^ step) for i in range(n)]
            x = x + lax.ppermute(x, a, pairs)
            step *= 2
    return x


def cent_sum(x):
    return doubling_sum(x, ("core", "cx"))


def dp_sum(x):
    n = lax.axis_size("dy") * lax.axis_size("dz")
    copies = jnp.broadcast_to(x[None], (n,) + x.shape)
    return jnp.sum(lax.all_to_all(copies, ("dy", "dz"), 0, 0, tiled=False), axis=0)


def doubling_gather(x, axis):
    n = lax.axis_size(axis)
    slots = jnp.zeros((n,) + x.shape, x.dtype)
    slots = lax.dynamic_update_index_in_dim(slots, x, lax.axis_index(axis), 0)
    return doubling_sum(slots, (axis,)).reshape((n * x.shape[0],) + x.shape[1:])


def row_update(boltzmann_affinity, column_factor):
    partial_rows = jnp.sum(boltzmann_affinity * column_factor[None, :], axis=1)
    return 1.0 / cent_sum(partial_rows)


def shards(embeddings, centroids):
    ny = lax.axis_size("dy")
    nz = lax.axis_size("dz")
    scaled_rows = normalize_wide(embeddings)
    normed = scaled_rows.astype(jnp.bfloat16)
    cent_normed = normalize(centroids)
    cosine_matches = lax.dot_general(
        normed, cent_normed, (((1,), (1,)), ((), ())), preferred_element_type=jnp.float32
    )
    boltzmann_affinity = jnp.exp(cosine_matches * (1.0 / (FEATURE_DIM * entropy_regularizer)))
    local_cents = centroids.shape[0]
    row_count = embeddings.shape[0] * ny * nz
    cent_count = local_cents * lax.axis_size("cx") * lax.axis_size("core")
    balance_ratio = row_count / cent_count
    column_factor = jnp.ones((local_cents,), jnp.float32)
    for sweep in range(ROUNDS):
        row_weight = row_update(boltzmann_affinity, column_factor)
        partial_cols = jnp.sum(row_weight[:, None] * boltzmann_affinity, axis=0)
        column_factor = balance_ratio / dp_sum(partial_cols)
    row_weight = row_update(boltzmann_affinity, column_factor)
    gathered = lax.all_gather(scaled_rows, "dy", axis=0, tiled=True)
    unit = column_factor[0] * 0.0 + 1.0
    gathered = (gathered * unit).astype(jnp.bfloat16)
    gathered_weight = doubling_gather(row_weight, "dy")
    sub_cents = local_cents // ny
    start = lax.axis_index("dy") * sub_cents
    sub_normed = lax.dynamic_slice_in_dim(cent_normed, start, sub_cents, 0)
    sub_factor = lax.dynamic_slice_in_dim(column_factor, start, sub_cents, 0)
    sub_matches = lax.dot_general(
        gathered, sub_normed, (((1,), (1,)), ((), ())), preferred_element_type=jnp.float32
    )
    sub_affinity = jnp.exp(sub_matches * (1.0 / (FEATURE_DIM * entropy_regularizer)))
    transport = (gathered_weight[:, None] * sub_affinity * sub_factor[None, :]).astype(
        jnp.bfloat16
    )
    col_mass = jnp.sum(transport, axis=0, dtype=jnp.float32)
    weighted = lax.dot_general(
        transport, gathered, (((0,), (0,)), ((), ())), preferred_element_type=jnp.float32
    )
    weighted, col_mass = lax.psum_scatter(
        (weighted, col_mass), "dz", scatter_dimension=0, tiled=True
    )
    return weighted / col_mass[:, None]


def split_mesh(mesh):
    devices = mesh.devices
    n_dp, n_cent = devices.shape
    try:
        ny = len({d.coords[1] for d in devices.flat})
        ncore = len({d.core_on_chip for d in devices.flat})
    except AttributeError:
        ny, ncore = 4, 2
    return Mesh(
        devices.reshape(ny, n_dp // ny, n_cent // ncore, ncore), ("dy", "dz", "cx", "core")
    )


def solution(mesh):
    sub = split_mesh(mesh)
    in_specs = (P(("dy", "dz"), None), P(("cx", "core"), None))
    out_specs = P(("cx", "core", "dy", "dz"), None)
    return jax.shard_map(shards, mesh=sub, in_specs=in_specs, out_specs=out_specs, check_vma=False)
```

```python
import jax
import jax.numpy as jnp
import numpy as np
from jax import lax
from jax.sharding import Mesh, PartitionSpec as P

FEATURE_DIM = 768
ROUNDS = 2


entropy_regularizer = 0.05


def normalize_wide(values):
    wide = values.astype(jnp.float32)
    meansq = jnp.mean(wide * wide, axis=-1, keepdims=True)
    return wide * lax.rsqrt(meansq + 1e-06)


def normalize(values):
    return normalize_wide(values).astype(jnp.bfloat16)


def doubling_sum(x, axes):
    for a in axes:
        n = lax.axis_size(a)
        step = 1
        while step < n:
            if 2 * step == n:
                pairs = [(i, n - 1 - i) for i in range(n)]
            else:
                pairs = [(i, i ^ step) for i in range(n)]
            x = x + lax.ppermute(x, a, pairs)
            step *= 2
    return x


def exchange_sum(x, axes):
    n = 1
    for a in axes:
        n *= lax.axis_size(a)
    copies = jnp.broadcast_to(x[None], (n,) + x.shape)
    return jnp.sum(lax.all_to_all(copies, axes, 0, 0, tiled=False), axis=0)


def cent_sum(x):
    return exchange_sum(x, ("cx", "core"))


def dp_sum(x):
    return exchange_sum(x, ("dy", "dz"))


def exchange_gather(x, axis):
    n = lax.axis_size(axis)
    copies = jnp.broadcast_to(x[None], (n,) + x.shape)
    blocks = lax.all_to_all(copies, axis, 0, 0, tiled=False)
    return blocks.reshape((n * x.shape[0],) + x.shape[1:])


def row_update(boltzmann_affinity, column_factor):
    partial_rows = jnp.sum(boltzmann_affinity * column_factor[None, :], axis=1)
    return 1.0 / cent_sum(partial_rows)


def shards(embeddings, centroids):
    ny = lax.axis_size("dy")
    nz = lax.axis_size("dz")
    scaled_rows = normalize_wide(embeddings)
    normed = scaled_rows.astype(jnp.bfloat16)
    cent_normed = normalize(centroids)
    cosine_matches = lax.dot_general(
        normed, cent_normed, (((1,), (1,)), ((), ())), preferred_element_type=jnp.float32
    )
    boltzmann_affinity = jnp.exp(cosine_matches * (1.0 / (FEATURE_DIM * entropy_regularizer)))
    local_cents = centroids.shape[0]
    row_count = embeddings.shape[0] * ny * nz
    cent_count = local_cents * lax.axis_size("cx") * lax.axis_size("core")
    balance_ratio = row_count / cent_count
    column_factor = jnp.ones((local_cents,), jnp.float32)
    for sweep in range(ROUNDS):
        row_weight = row_update(boltzmann_affinity, column_factor)
        partial_cols = jnp.sum(row_weight[:, None] * boltzmann_affinity, axis=0)
        column_factor = balance_ratio / dp_sum(partial_cols)
    row_weight = row_update(boltzmann_affinity, column_factor)
    gathered = lax.all_gather(scaled_rows, "dy", axis=0, tiled=True)
    unit = column_factor[0] * 0.0 + 1.0
    gathered = (gathered * unit).astype(jnp.bfloat16)
    gathered_weight = exchange_gather(row_weight, "dy")
    sub_cents = local_cents // ny
    start = lax.axis_index("dy") * sub_cents
    sub_normed = lax.dynamic_slice_in_dim(cent_normed, start, sub_cents, 0)
    sub_factor = lax.dynamic_slice_in_dim(column_factor, start, sub_cents, 0)
    sub_matches = lax.dot_general(
        gathered, sub_normed, (((1,), (1,)), ((), ())), preferred_element_type=jnp.float32
    )
    sub_affinity = jnp.exp(sub_matches * (1.0 / (FEATURE_DIM * entropy_regularizer)))
    transport = (gathered_weight[:, None] * sub_affinity * sub_factor[None, :]).astype(
        jnp.bfloat16
    )
    col_mass = jnp.sum(transport, axis=0, dtype=jnp.float32)
    weighted = lax.dot_general(
        transport, gathered, (((0,), (0,)), ((), ())), preferred_element_type=jnp.float32
    )
    weighted, col_mass = lax.psum_scatter(
        (weighted, col_mass), "dz", scatter_dimension=0, tiled=True
    )
    return weighted / col_mass[:, None]


def split_mesh(mesh):
    devices = mesh.devices
    n_dp, n_cent = devices.shape
    try:
        ny = len({d.coords[1] for d in devices.flat})
        ncore = len({d.core_on_chip for d in devices.flat})
    except AttributeError:
        ny, ncore = 4, 2
    return Mesh(
        devices.reshape(ny, n_dp // ny, n_cent // ncore, ncore), ("dy", "dz", "cx", "core")
    )


def solution(mesh):
    sub = split_mesh(mesh)
    in_specs = (P(("dy", "dz"), None), P(("cx", "core"), None))
    out_specs = P(("cx", "core", "dy", "dz"), None)
    return jax.shard_map(shards, mesh=sub, in_specs=in_specs, out_specs=out_specs, check_vma=False)
```

```python
import jax
import jax.numpy as jnp
import numpy as np
from jax import lax
from jax.sharding import Mesh, PartitionSpec as P

FEATURE_DIM = 768
ROUNDS = 2


entropy_regularizer = 0.05


def normalize_wide(values):
    wide = values.astype(jnp.float32)
    meansq = jnp.mean(wide * wide, axis=-1, keepdims=True)
    return wide * lax.rsqrt(meansq + 1e-06)


def normalize(values):
    return normalize_wide(values).astype(jnp.bfloat16)


def doubling_sum(x, axes):
    for a in axes:
        n = lax.axis_size(a)
        step = 1
        while step < n:
            if 2 * step == n:
                pairs = [(i, n - 1 - i) for i in range(n)]
            else:
                pairs = [(i, i ^ step) for i in range(n)]
            x = x + lax.ppermute(x, a, pairs)
            step *= 2
    return x


def cent_sum(x):
    return doubling_sum(x, ("core", "cx"))


def dp_sum(x):
    n = lax.axis_size("dy") * lax.axis_size("dz")
    copies = jnp.broadcast_to(x[None], (n,) + x.shape)
    return jnp.sum(lax.all_to_all(copies, ("dy", "dz"), 0, 0, tiled=False), axis=0)


def exchange_gather(x, axis):
    n = lax.axis_size(axis)
    copies = jnp.broadcast_to(x[None], (n,) + x.shape)
    blocks = lax.all_to_all(copies, axis, 0, 0, tiled=False)
    return blocks.reshape((n * x.shape[0],) + x.shape[1:])


def row_update(boltzmann_affinity, column_factor):
    partial_rows = jnp.sum(boltzmann_affinity * column_factor[None, :], axis=1)
    return 1.0 / cent_sum(partial_rows)


def shards(embeddings, centroids):
    ny = lax.axis_size("dy")
    nz = lax.axis_size("dz")
    scaled_rows = normalize_wide(embeddings)
    normed = scaled_rows.astype(jnp.bfloat16)
    cent_normed = normalize(centroids)
    cosine_matches = lax.dot_general(
        normed, cent_normed, (((1,), (1,)), ((), ())), preferred_element_type=jnp.float32
    )
    boltzmann_affinity = jnp.exp(cosine_matches * (1.0 / (FEATURE_DIM * entropy_regularizer)))
    local_cents = centroids.shape[0]
    row_count = embeddings.shape[0] * ny * nz
    cent_count = local_cents * lax.axis_size("cx") * lax.axis_size("core")
    balance_ratio = row_count / cent_count
    column_factor = jnp.ones((local_cents,), jnp.float32)
    for sweep in range(ROUNDS):
        row_weight = row_update(boltzmann_affinity, column_factor)
        partial_cols = jnp.sum(row_weight[:, None] * boltzmann_affinity, axis=0)
        column_factor = balance_ratio / dp_sum(partial_cols)
    row_weight = row_update(boltzmann_affinity, column_factor)
    gathered = lax.all_gather(scaled_rows, "dy", axis=0, tiled=True)
    unit = column_factor[0] * 0.0 + 1.0
    gathered = (gathered * unit).astype(jnp.bfloat16)
    gathered_weight = exchange_gather(row_weight, "dy")
    sub_cents = local_cents // ny
    start = lax.axis_index("dy") * sub_cents
    sub_normed = lax.dynamic_slice_in_dim(cent_normed, start, sub_cents, 0)
    sub_factor = lax.dynamic_slice_in_dim(column_factor, start, sub_cents, 0)
    sub_matches = lax.dot_general(
        gathered, sub_normed, (((1,), (1,)), ((), ())), preferred_element_type=jnp.float32
    )
    sub_affinity = jnp.exp(sub_matches * (1.0 / (FEATURE_DIM * entropy_regularizer)))
    transport = (gathered_weight[:, None] * sub_affinity * sub_factor[None, :]).astype(
        jnp.bfloat16
    )
    col_mass = jnp.sum(transport, axis=0, dtype=jnp.float32)
    weighted = lax.dot_general(
        transport, gathered, (((0,), (0,)), ((), ())), preferred_element_type=jnp.float32
    )
    weighted, col_mass = lax.psum_scatter(
        (weighted, col_mass), "dz", scatter_dimension=0, tiled=True
    )
    return weighted / col_mass[:, None]


def split_mesh(mesh):
    devices = mesh.devices
    n_dp, n_cent = devices.shape
    try:
        ny = len({d.coords[1] for d in devices.flat})
        ncore = len({d.core_on_chip for d in devices.flat})
    except AttributeError:
        ny, ncore = 4, 2
    return Mesh(
        devices.reshape(ny, n_dp // ny, n_cent // ncore, ncore), ("dy", "dz", "cx", "core")
    )


def solution(mesh):
    sub = split_mesh(mesh)
    in_specs = (P(("dy", "dz"), None), P(("cx", "core"), None))
    out_specs = P(("cx", "core", "dy", "dz"), None)
    return jax.shard_map(shards, mesh=sub, in_specs=in_specs, out_specs=out_specs, check_vma=False)
```

```python
import jax
import jax.numpy as jnp
import numpy as np
from jax import lax
from jax.sharding import Mesh, PartitionSpec as P

FEATURE_DIM = 768
ROUNDS = 2


entropy_regularizer = 0.05


def normalize_wide(values):
    wide = values.astype(jnp.float32)
    meansq = jnp.mean(wide * wide, axis=-1, keepdims=True)
    return wide * lax.rsqrt(meansq + 1e-06)


def normalize(values):
    return normalize_wide(values).astype(jnp.bfloat16)


def doubling_sum(x, axes):
    for a in axes:
        n = lax.axis_size(a)
        step = 1
        while step < n:
            if 2 * step == n:
                pairs = [(i, n - 1 - i) for i in range(n)]
            else:
                pairs = [(i, i ^ step) for i in range(n)]
            x = x + lax.ppermute(x, a, pairs)
            step *= 2
    return x


def cent_sum(x):
    return doubling_sum(x, ("core", "cx"))


def dp_sum(x):
    n = lax.axis_size("dy") * lax.axis_size("dz")
    copies = jnp.broadcast_to(x[None], (n,) + x.shape)
    return jnp.sum(lax.all_to_all(copies, ("dy", "dz"), 0, 0, tiled=False), axis=0)


def doubling_gather(x, axis):
    n = lax.axis_size(axis)
    slots = jnp.zeros((n,) + x.shape, x.dtype)
    slots = lax.dynamic_update_index_in_dim(slots, x, lax.axis_index(axis), 0)
    return doubling_sum(slots, (axis,)).reshape((n * x.shape[0],) + x.shape[1:])


def row_update(boltzmann_affinity, column_factor):
    partial_rows = jnp.sum(boltzmann_affinity * column_factor[None, :], axis=1)
    return 1.0 / cent_sum(partial_rows)


def shards(embeddings, centroids):
    ny = lax.axis_size("dy")
    nz = lax.axis_size("dz")
    scaled_rows = normalize_wide(embeddings)
    normed = scaled_rows.astype(jnp.bfloat16)
    cent_normed = normalize(centroids)
    cosine_matches = lax.dot_general(
        normed, cent_normed, (((1,), (1,)), ((), ())), preferred_element_type=jnp.float32
    )
    boltzmann_affinity = jnp.exp(cosine_matches * (1.0 / (FEATURE_DIM * entropy_regularizer)))
    local_cents = centroids.shape[0]
    row_count = embeddings.shape[0] * ny * nz
    cent_count = local_cents * lax.axis_size("cx") * lax.axis_size("core")
    balance_ratio = row_count / cent_count
    column_factor = jnp.ones((local_cents,), jnp.float32)
    for sweep in range(ROUNDS):
        row_weight = row_update(boltzmann_affinity, column_factor)
        partial_cols = jnp.sum(row_weight[:, None] * boltzmann_affinity, axis=0)
        column_factor = balance_ratio / dp_sum(partial_cols)
    partial_rows = jnp.sum(boltzmann_affinity * column_factor[None, :], axis=1)
    slots = jnp.zeros((ny,) + partial_rows.shape, jnp.float32)
    slots = lax.dynamic_update_index_in_dim(slots, partial_rows, lax.axis_index("dy"), 0)
    copies = jnp.broadcast_to(slots[None], (ny * lax.axis_size("cx") * lax.axis_size("core"),) + slots.shape)
    row_totals = jnp.sum(lax.all_to_all(copies, ("dy", "cx", "core"), 0, 0, tiled=False), axis=0)
    gathered = lax.all_gather(scaled_rows, "dy", axis=0, tiled=True)
    unit = column_factor[0] * 0.0 + 1.0
    gathered = (gathered * unit).astype(jnp.bfloat16)
    gathered_weight = (1.0 / row_totals).reshape(-1)
    sub_cents = local_cents // ny
    start = lax.axis_index("dy") * sub_cents
    sub_normed = lax.dynamic_slice_in_dim(cent_normed, start, sub_cents, 0)
    sub_factor = lax.dynamic_slice_in_dim(column_factor, start, sub_cents, 0)
    sub_matches = lax.dot_general(
        gathered, sub_normed, (((1,), (1,)), ((), ())), preferred_element_type=jnp.float32
    )
    sub_affinity = jnp.exp(sub_matches * (1.0 / (FEATURE_DIM * entropy_regularizer)))
    transport = (gathered_weight[:, None] * sub_affinity * sub_factor[None, :]).astype(
        jnp.bfloat16
    )
    col_mass = jnp.sum(transport, axis=0, dtype=jnp.float32)
    weighted = lax.dot_general(
        transport, gathered, (((0,), (0,)), ((), ())), preferred_element_type=jnp.float32
    )
    weighted, col_mass = lax.psum_scatter(
        (weighted, col_mass), "dz", scatter_dimension=0, tiled=True
    )
    return weighted / col_mass[:, None]


def split_mesh(mesh):
    devices = mesh.devices
    n_dp, n_cent = devices.shape
    try:
        ny = len({d.coords[1] for d in devices.flat})
        ncore = len({d.core_on_chip for d in devices.flat})
    except AttributeError:
        ny, ncore = 4, 2
    return Mesh(
        devices.reshape(ny, n_dp // ny, n_cent // ncore, ncore), ("dy", "dz", "cx", "core")
    )


def solution(mesh):
    sub = split_mesh(mesh)
    in_specs = (P(("dy", "dz"), None), P(("cx", "core"), None))
    out_specs = P(("cx", "core", "dy", "dz"), None)
    return jax.shard_map(shards, mesh=sub, in_specs=in_specs, out_specs=out_specs, check_vma=False)
```
